256 devices in a mesh: set: 32 (over y, x, core), path: 8 (over z).
Axes of the slice: x: 4, y: 4, z: 8, core: 2. Of those that a mesh axis runs over, the one named last changes fastest.
Arguments:
- start_state: float32 [4096, 2048], P(('path', 'set')), may hold values from -6 to 6
- shocks: bfloat16 [2, 4096, 2048], P(None, ('path', 'set')), may hold values from -6 to 6
- loading: bfloat16 [2048, 2048], replicated, may hold values from -0.125 to 0.125
- decay: float32 [2048], replicated, may hold values from 0.5 to 1
- factor_lists: int32 [4096, 64], P('set'), may hold values from 0 to 2047, all different within a row
- delta: bfloat16 [4096, 64], P('set'), may hold values from -0.75 to 0.75
- gamma: bfloat16 [4096, 64, 64], P('set'), may hold values from -0.09375 to 0.09375
- currency: int32 [4096], P('set'), may hold values from 0 to 15
- owner: int32 [4096], P('set'), may hold values from 0 to 255
Outputs:
- exposure: float32 [2, 256, 4096], P(None, 'set', 'path')
- end_state: float32 [4096, 2048], P(('path', 'set'))
The draws below stay inside these ranges and needn't reach their ends.
Inputs may be any that keep to these rules, and one draw needn't show every extreme that they name: `factor_lists`: the 64 factors of one netting set are different.
All inputs are finite; a program needn't handle non-finite values.
Results may differ from the reference program's by a relative error of at most 0.004.
Values may be sent and summed in bfloat16 or wider, within the bound.
No kernel may reach another device: no remote copies, remote signals or barrier semaphores. Data moves between devices by JAX's collectives and lax.ppermute only.
A program may use at most 64 MiB of HBM per device.

```python
import math
import jax
import jax.numpy as jnp
import numpy as np
from jax import lax

F = 2048
K = 64
NB = 16
NCUR = 16
STEPS = 2
PATHS = 4096
SETS = 4096
CPS = 256


def place_ends(drawn, rng, low, high):
    longest = drawn.shape.index(max(drawn.shape))
    spots = []
    for shift in (0, 1):
        where = [jax.random.randint(jax.random.fold_in(rng, axis), (), 0, length) for axis, length in enumerate(drawn.shape)]
        where[longest] = (where[longest] + shift) % drawn.shape[longest]
        spots.append(tuple(where))
    return drawn.at[spots[0]].set(low).at[spots[1]].set(high)


def block_levels(key, shape, pieces, smallest, top_value):
    gain = 1.0
    for axis_at, parts in pieces:
        draws = jax.random.uniform(jax.random.fold_in(jax.random.fold_in(key, 6), axis_at), (parts,), jnp.float32, smallest / len(pieces), top_value / len(pieces))
        gain = gain * jnp.repeat(jnp.exp(draws), shape[axis_at] // parts).reshape((-1,) + (1,) * (len(shape) - 1 - axis_at))
    return gain


def rank_table(count, lean):
    weights = [(1 << 20) // math.isqrt(grade ** lean) + 1 for grade in range(1, count + 1)]
    deviation = 1 + sum(weights) // (1 << 30)
    return np.cumsum(np.array([max(1, weight // deviation) for weight in weights]))


def ranked(rng, extent, number_of, lean):
    listing = rank_table(number_of, lean)
    lot = jax.random.randint(jax.random.fold_in(rng, 1), extent, 0, int(listing[number_of - 1]))
    rank = jnp.searchsorted(jnp.asarray(listing, jnp.int32), lot, side="right")
    return jax.random.permutation(jax.random.fold_in(rng, 2), number_of)[rank].astype(jnp.int32)


def choose_distinct(stream_key, rows, amount, top, lift):
    sequence = jax.random.permutation(jax.random.fold_in(stream_key, 1), amount)
    pull = sequence
    for power in range(3):
        pull = pull * pull // amount
    pull = pull * lift // amount
    chance = jax.random.randint(jax.random.fold_in(stream_key, 2), (rows, amount), 0, 4096) + pull
    sure = jax.random.permutation(jax.random.fold_in(stream_key, 3), rows)[jnp.arange(amount) % rows]
    chance = jnp.where(jnp.arange(rows)[:, None] == sure[None, :], 1 << 14, chance)
    priority = chance * amount + jnp.arange(amount)
    return lax.top_k(priority.astype(jnp.int32), top)[1].astype(jnp.int32)


def bell_draw(key, extent, scale, most, cuts=(), kind=jnp.bfloat16):
    level = block_levels(key, extent, cuts, -0.22, 0.18) if cuts else 1.0
    result = jax.random.normal(key, extent, jnp.float32) * scale * level
    return jnp.minimum(jnp.maximum(result, -most), most).astype(kind)


def setup_inputs(seed: int = 0) -> dict:
    key_of = jax.random.split(jax.random.key(seed), 10)
    start_state = bell_draw(key_of[0], (PATHS, F), 1.0, 6.0, ((0, 256),), jnp.float32)
    shocks = bell_draw(key_of[1], (STEPS, PATHS, F), 1.0, 6.0, ((1, 256),))
    loading = bell_draw(key_of[2], (F, F), F ** -0.5, 0.125)
    decay = jnp.clip(jax.random.uniform(key_of[3], (F,), jnp.float32, 0.5, 1.0), 0.5, 1.0)
    factor_lists = choose_distinct(key_of[4], SETS, F, K, 512)
    delta = bell_draw(key_of[5], (SETS, K), K ** -0.5, 0.75, ((0, 32),))
    gamma = bell_draw(key_of[6], (SETS, K, K), (K * K) ** -0.5, 0.09375, ((0, 32),))
    currency = place_ends(jax.random.randint(key_of[7], (SETS,), 0, NCUR), jax.random.fold_in(key_of[7], 1), 0, NCUR - 1).astype(jnp.int32)
    owner = place_ends(ranked(key_of[8], (SETS,), CPS, 2), jax.random.fold_in(key_of[8], 3), 0, CPS - 1).astype(jnp.int32)
    return dict(start_state=start_state, shocks=shocks, loading=loading, decay=decay, factor_lists=factor_lists, delta=delta, gamma=gamma, currency=currency, owner=owner)


def value_block(slab, lists_b, delta_b, gamma_b, cur_b):
    rows = slab.shape[0]
    count = lists_b.shape[0]
    picked = jnp.take(slab, lists_b.reshape(-1), axis=1).reshape(rows, count, lists_b.shape[1])
    curved = jnp.einsum('psk,skl->psl', picked.astype(jnp.float32), gamma_b.astype(jnp.float32))
    linear = delta_b.astype(jnp.float32)[None] + 0.5 * curved
    local = jnp.sum(picked.astype(jnp.float32) * linear, axis=2)
    rates = jnp.exp(0.2 * jnp.take(slab, cur_b, axis=1).astype(jnp.float32))
    return (local * rates).T

def revalue(slab, lists, delta, gamma, cur):
    total = lists.shape[0]
    width = math.gcd(16, total)
    blocks = total // width
    depth = lists.shape[1]
    stacked = lax.map(lambda a: value_block(slab, a[0], a[1], a[2], a[3]), (lists.reshape(blocks, width, depth), delta.reshape(blocks, width, depth), gamma.reshape(blocks, width, depth, depth), cur.reshape(blocks, width)))
    return stacked.reshape(total, slab.shape[0])

def regress(gram, moments, total):
    size = gram.shape[0]
    chol = jnp.linalg.cholesky(gram / total + 0.001 * jnp.eye(size, dtype=jnp.float32))
    middle = lax.linalg.triangular_solve(chol, moments / total, left_side=True, lower=True)
    return lax.linalg.triangular_solve(chol, middle, left_side=True, lower=True, transpose_a=True)

def reference(start_state, shocks, loading, decay, factor_lists, delta, gamma, currency, owner):
    high = lax.Precision.HIGHEST
    onehot = (owner[None, :] == jnp.arange(CPS, dtype=jnp.int32)[:, None]).astype(jnp.float32)
    state = start_state
    results = []
    for step in range(STEPS):
        state = decay[None, :] * state + jnp.dot(shocks[step].astype(jnp.float32), loading.astype(jnp.float32), preferred_element_type=jnp.float32)
        slab = state.astype(jnp.bfloat16)
        values = revalue(slab, factor_lists, delta, gamma, currency)
        netted = jnp.dot(onehot, values, precision=high)
        ones = jnp.ones((1, slab.shape[0]), jnp.float32)
        basis = jnp.concatenate([ones, slab[:, :NB].astype(jnp.float32).T], axis=0)
        gram = jnp.dot(basis, basis.T, precision=high)
        moments = jnp.dot(basis, netted.T, precision=high)
        coef = regress(gram, moments, PATHS)
        fitted = jnp.dot(coef.T, basis, precision=high)
        results.append(jnp.maximum(netted - 0.9 * fitted, 0.0))
    return (jnp.stack(results), state)
```

```python
import jax
import jax.numpy as jnp
from jax import lax
from jax.experimental import pallas as pl
from jax.experimental.pallas import tpu as pltpu
from jax.sharding import PartitionSpec as P

F32 = jnp.float32
BF16 = jnp.bfloat16
HIGH = lax.Precision.HIGHEST

NB = 16
STEPS = 2
ROWS = 16
LANES = 128
GRID = 4
HOPS = (0, 1, 3, 2)
NG = 4
PITCH = 9
SUB = 8
NBP = 24


def chip_index(y, x, core):
    return (y * GRID + x) * 2 + core


def hop_pairs(hop, flip):
    pairs = []
    for y in range(GRID):
        for x in range(GRID):
            for core in range(2):
                if core ^ flip == 0:
                    to = chip_index(y, (x + hop) % GRID, core)
                else:
                    to = chip_index((y + hop) % GRID, x, core)
                pairs.append((chip_index(y, x, core), to))
    return pairs


def core_pairs():
    return [(i, i ^ 1) for i in range(2 * GRID * GRID)]


def prepare(gamma, delta):
    sets, depth, _ = gamma.shape
    wide = NG * depth
    per = 4

    def body(g_ref, d_ref, o_ref):
        zero = jnp.zeros((depth, depth), F32)
        row = lax.broadcasted_iota(jnp.int32, (16, depth), 0)
        for b in range(per):
            for i in range(NG):
                j = b * NG + i
                g = g_ref[j].astype(F32) * 0.5
                parts = [g if k == i else zero for k in range(NG)]
                o_ref[b, i * depth:(i + 1) * depth, :] = jnp.concatenate(parts, axis=1).astype(BF16)
            d = [d_ref[b * NG + i:b * NG + i + 1, :].astype(F32) for i in range(NG)]
            tail = [jnp.where(row == i, jnp.broadcast_to(d[i], (16, depth)), 0.0) for i in range(NG)]
            o_ref[b, wide:, :] = jnp.concatenate(tail, axis=1).astype(BF16)

    return pl.pallas_call(
        body,
        grid=(sets // (NG * per),),
        in_specs=[
            pl.BlockSpec((NG * per, depth, depth), lambda i: (i, 0, 0)),
            pl.BlockSpec((NG * per, depth), lambda i: (i, 0)),
        ],
        out_specs=pl.BlockSpec((per, wide + 16, wide), lambda i: (i, 0, 0)),
        out_shape=jax.ShapeDtypeStruct((sets // NG, wide + 16, wide), BF16),
        name="prepare",
    )(gamma, delta)


def revalue(slots, lists, currency, owner, arrays, gd, sets, depth):
    factors = arrays[0].shape[1]
    blocks = arrays[0].shape[0] // (STEPS * ROWS)
    sources = len(arrays) * blocks
    chunks = sources * ROWS // LANES
    per_chunk = LANES // ROWS
    groups = sets // NG
    wide = NG * depth
    counterparties = 2 * 128
    tile = 256

    def body(slots, lists, cur, own, *refs):
        arrs = refs[:len(arrays)]
        gd_hbm, mine, theirs, base = refs[len(arrays):len(arrays) + 4]
        sl, st, xa, xb, rates, gdv, net, sem, gsem, osem = refs[len(arrays) + 4:]
        copies = []
        for a in range(len(arrays)):
            for e in range(blocks):
                n = a * blocks + e
                cp = pltpu.make_async_copy(
                    arrs[a].at[pl.ds(e * STEPS * ROWS, STEPS * ROWS), :], sl.at[slots[n]], sem.at[n]
                )
                cp.start()
                copies.append(cp)
        gcp = pltpu.make_async_copy(gd_hbm, gdv, gsem)
        gcp.start()
        net[...] = jnp.zeros(net.shape, F32)
        for cp in copies:
            cp.wait()

        def turn(ft, carry):
            f0 = pl.multiple_of(ft * tile, tile)
            for t in range(STEPS):
                for q in range(chunks):
                    blk = sl[pl.ds(per_chunk * q, per_chunk), pl.ds(t * ROWS, ROWS), pl.ds(f0, tile)]
                    o = jnp.transpose(blk.reshape(LANES, tile).astype(F32))
                    st[pl.ds(f0 * SUB + (t * chunks + q), tile, stride=SUB), :] = o
            return carry

        lax.fori_loop(0, factors // tile, turn, 0)
        for c in range(NB):
            b = st[pl.ds(c * SUB, SUB), :]
            base[pl.ds(c * SUB, SUB), :] = b
            rates[c] = jnp.exp(0.2 * b)

        def picks(j, x, k0, k1):
            for k in range(k0, k1):
                i = lists.at[pl.ds(k * groups, groups)][j]
                x[pl.ds(k * PITCH, SUB), :] = st[pl.ds(pl.multiple_of(i, SUB), SUB), :]

        sub = lax.broadcasted_iota(jnp.int32, (SUB, LANES), 0)
        halves = SUB // 2

        def value(j, x, jn, xn):
            g = gdv[j]
            loc = [jnp.zeros((SUB, LANES), F32) for _ in range(NG)]
            for p in range(halves):
                picks(jn, xn, wide * p // halves, wide * (p + 1) // halves)
                xs = jnp.concatenate(
                    [x[pl.ds(2 * p, wide, stride=PITCH), :], x[pl.ds(2 * p + 1, wide, stride=PITCH), :]], axis=1
                )
                o = jnp.dot(g, xs.astype(BF16), preferred_element_type=F32)
                for i in range(NG):
                    y = xs[i * depth:(i + 1) * depth] * o[i * depth:(i + 1) * depth]
                    r = jnp.sum(y, axis=0, keepdims=True) + o[wide + i:wide + i + 1]
                    loc[i] = jnp.where(sub == 2 * p, r[:, :LANES], loc[i])
                    loc[i] = jnp.where(sub == 2 * p + 1, r[:, LANES:], loc[i])
            for i in range(NG):
                s = j * NG + i
                c = own[s]
                net[c] = net[c] + loc[i] * rates[cur[s]]

        gcp.wait()
        picks(0, xa, 0, wide)

        def loop(jj, carry):
            j = jj * 2
            value(j, xa, j + 1, xb)
            value(j + 1, xb, jnp.minimum(j + 2, groups - 1), xa)
            return carry

        lax.fori_loop(0, groups // 2, loop, 0)
        half = counterparties // 2
        outs = [
            pltpu.make_async_copy(net.at[pl.ds(half, half)], theirs, osem.at[0]),
            pltpu.make_async_copy(net.at[pl.ds(0, half)], mine, osem.at[1]),
        ]
        for cp in outs:
            cp.start()
        for cp in outs:
            cp.wait()

    smem = pl.BlockSpec(memory_space=pltpu.SMEM)
    hbm = pl.BlockSpec(memory_space=pltpu.HBM)
    vmem = pl.BlockSpec(memory_space=pltpu.VMEM)
    half_shape = jax.ShapeDtypeStruct((counterparties // 2, SUB, LANES), F32)
    return pl.pallas_call(
        body,
        in_specs=[smem] * 4 + [hbm] * (len(arrays) + 1),
        out_specs=(hbm, hbm, vmem),
        out_shape=(half_shape, half_shape, jax.ShapeDtypeStruct((NB * SUB, LANES), F32)),
        scratch_shapes=[
            pltpu.VMEM((sources, STEPS * ROWS, factors), BF16),
            pltpu.VMEM((factors * SUB, LANES), F32),
            pltpu.VMEM((wide * PITCH, LANES), F32),
            pltpu.VMEM((wide * PITCH, LANES), F32),
            pltpu.VMEM((NB, SUB, LANES), F32),
            pltpu.VMEM(gd.shape, BF16),
            pltpu.VMEM((counterparties, SUB, LANES), F32),
            pltpu.SemaphoreType.DMA((sources,)),
            pltpu.SemaphoreType.DMA(()),
            pltpu.SemaphoreType.DMA((2,)),
        ],
        compiler_params=pltpu.CompilerParams(vmem_limit_bytes=40 * 1024 * 1024),
        name="revalue",
    )(slots, lists, currency, owner, *[pltpu.with_memory_space_constraint(a, pltpu.HBM) for a in (*arrays, gd)])


def basis_rows(base, s):
    row = lax.broadcasted_iota(jnp.int32, (NBP - NB, LANES), 0)
    one = jnp.where(row == 0, 1.0, 0.0).astype(F32)
    return jnp.concatenate([base[pl.ds(s, NB, stride=SUB), :], one], axis=0)


def moments_of(parts, base):
    chunks = SUB // STEPS

    def body(p_ref, b_ref, net_ref, out_ref):
        net_ref[...] = jnp.sum(p_ref[...], axis=0)
        out_ref[...] = jnp.zeros(out_ref.shape, F32)
        for t in range(STEPS):
            left, right = [], []
            for q in range(chunks):
                s = t * chunks + q
                b = basis_rows(b_ref, s)
                right.append(b)
                left.append(jnp.concatenate([b, net_ref[pl.ds(s, SUB, stride=SUB), :]], axis=0))
            m = lax.dot_general(
                jnp.concatenate(left, axis=1), jnp.concatenate(right, axis=1), (((1,), (1,)), ((), ())),
                precision=HIGH, preferred_element_type=F32,
            )
            out_ref[t, :, 0:NBP] = m

    return pl.pallas_call(
        body,
        out_shape=(
            jax.ShapeDtypeStruct((SUB * SUB, LANES), F32),
            jax.ShapeDtypeStruct((STEPS, NBP + SUB, LANES), F32),
        ),
        name="moments",
    )(parts, base)


def expose(payload, net, base, total):
    chunks = SUB // STEPS

    def body(p_ref, n_ref, b_ref, o_ref):
        acc = jnp.sum(p_ref[...], axis=0) * (1.0 / total)
        row = lax.broadcasted_iota(jnp.int32, (NBP + SUB, LANES), 0)
        lane = lax.broadcasted_iota(jnp.int32, (NBP + SUB, LANES), 1)
        diag = jnp.where((row == lane) & (row < NBP), jnp.where(row <= NB, 0.001, 1.0), 0.0)
        sys = [acc[t] + diag for t in range(STEPS)]
        for k in range(NB + 1):
            for t in range(STEPS):
                a = sys[t]
                r = a[k:k + 1, :]
                c = a[:, k:k + 1] / a[k:k + 1, k:k + 1]
                sys[t] = jnp.where(lane == k, c, a - c * r)
        for t in range(STEPS):
            coef = sys[t][NBP:, 0:NBP]
            for q in range(chunks):
                s = t * chunks + q
                fitted = jnp.dot(coef, basis_rows(b_ref, s), precision=HIGH, preferred_element_type=F32)
                n = n_ref[pl.ds(s, SUB, stride=SUB), :]
                o_ref[t, :, q * LANES:(q + 1) * LANES] = jnp.maximum(n - 0.9 * fitted, 0.0)

    return pl.pallas_call(
        body,
        out_shape=jax.ShapeDtypeStruct((STEPS, SUB, chunks * LANES), F32),
        name="expose",
    )(payload, net, base)


def per_device(start_state, shocks, loading, decay, factor_lists, delta, gamma, currency, owner):
    member = lax.axis_index("set")
    core, px, py = member % 2, (member // 2) % GRID, member // (2 * GRID)
    sets, depth = factor_lists.shape
    total = ROWS * lax.axis_size("set") * lax.axis_size("path")
    factors = start_state.shape[1]

    moved = jnp.dot(shocks.reshape(STEPS * ROWS, factors), loading, preferred_element_type=F32)
    first = decay[None, :] * start_state + moved[:ROWS]
    state = decay[None, :] * first + moved[ROWS:]
    slab = jnp.concatenate([first, state], axis=0).astype(BF16)

    line = [slab] + [lax.ppermute(slab, "set", hop_pairs(h, 0)) for h in HOPS[1:]]
    line = jnp.concatenate(line, axis=0)
    plane = [line] + [lax.ppermute(line, "set", hop_pairs(h, 1)) for h in HOPS[1:]]
    other = [lax.ppermute(a, "set", core_pairs()) for a in plane]

    hops = jnp.array(HOPS, jnp.int32)
    near, far = hops[None, :], hops[:, None]

    def slots_of(c):
        dx = jnp.where(c == 0, near, far)
        dy = jnp.where(c == 0, far, near)
        return (((py - dy) % GRID * GRID + (px - dx) % GRID) * 2 + c).reshape(-1)

    slots = jnp.concatenate([slots_of(core), slots_of(1 - core)]).astype(jnp.int32)
    lists = (factor_lists * SUB).reshape(sets // NG, NG * depth).T.reshape(-1)
    place = jnp.where((owner // SUB) % 2 == core, 0, 128) + owner // (2 * SUB) * SUB + owner % SUB

    gd = prepare(gamma, delta)
    mine, theirs, base = revalue(slots, lists, currency, place, plane + other, gd, sets, depth)
    mine = mine + lax.ppermute(theirs, "set", core_pairs())
    chips = [[i * 2 + c for i in range(GRID * GRID)] for c in range(2)]
    parts = lax.all_to_all(
        mine.reshape(GRID * GRID, SUB * SUB, LANES), "set", 0, 0, axis_index_groups=chips
    )
    net, payload = moments_of(parts, base)
    paths = lax.axis_size("path")
    payload = lax.all_to_all(jnp.broadcast_to(payload[None], (paths,) + payload.shape), "path", 0, 0)
    return expose(payload, net, base, total), state


def solution(mesh):
    return jax.shard_map(
        per_device,
        mesh=mesh,
        in_specs=(
            P(("path", "set"), None),
            P(None, ("path", "set"), None),
            P(),
            P(),
            P("set", None),
            P("set", None),
            P("set", None, None),
            P("set"),
            P("set"),
        ),
        out_specs=(P(None, "set", "path"), P(("path", "set"), None)),
        check_vma=False,
    )
```

```python
import jax
import jax.numpy as jnp
from jax import lax
from jax.experimental import pallas as pl
from jax.experimental.pallas import tpu as pltpu
from jax.sharding import PartitionSpec as P

F32 = jnp.float32
BF16 = jnp.bfloat16
HIGH = lax.Precision.HIGHEST

NB = 16
STEPS = 2
ROWS = 16
LANES = 128
GRID = 4
HOPS = (0, 1, 3, 2)
NG = 4
PITCH = 9
SUB = 8
VMEM_SPEC = pl.BlockSpec(memory_space=pltpu.VMEM)
NBP = 24


def on_chip(a):
    return pltpu.with_memory_space_constraint(a, pltpu.VMEM)


def chip_index(y, x, core):
    return (y * GRID + x) * 2 + core


def hop_pairs(hop, flip):
    pairs = []
    for y in range(GRID):
        for x in range(GRID):
            for core in range(2):
                if core ^ flip == 0:
                    to = chip_index(y, (x + hop) % GRID, core)
                else:
                    to = chip_index((y + hop) % GRID, x, core)
                pairs.append((chip_index(y, x, core), to))
    return pairs


def core_pairs():
    return [(i, i ^ 1) for i in range(2 * GRID * GRID)]


def prepare(gamma, delta):
    sets, depth, _ = gamma.shape
    wide = NG * depth
    per = 16

    def body(g_ref, d_ref, o_ref):
        zero = jnp.zeros((depth, depth), F32)
        row = lax.broadcasted_iota(jnp.int32, (16, depth), 0)
        for b in range(per):
            for i in range(NG):
                j = b * NG + i
                g = g_ref[j].astype(F32) * 0.5
                parts = [g if k == i else zero for k in range(NG)]
                o_ref[b, i * depth:(i + 1) * depth, :] = jnp.concatenate(parts, axis=1).astype(BF16)
            d = [d_ref[b * NG + i:b * NG + i + 1, :].astype(F32) for i in range(NG)]
            tail = [jnp.where(row == i, jnp.broadcast_to(d[i], (16, depth)), 0.0) for i in range(NG)]
            o_ref[b, wide:, :] = jnp.concatenate(tail, axis=1).astype(BF16)

    return pl.pallas_call(
        body,
        grid=(sets // (NG * per),),
        in_specs=[
            pl.BlockSpec((NG * per, depth, depth), lambda i: (i, 0, 0)),
            pl.BlockSpec((NG * per, depth), lambda i: (i, 0)),
        ],
        out_specs=pl.BlockSpec((per, wide + 16, wide), lambda i: (i, 0, 0)),
        out_shape=jax.ShapeDtypeStruct((sets // NG, wide + 16, wide), BF16),
        name="prepare",
    )(gamma, delta)


def revalue(slots, lists, currency, owner, arrays, gd, sets, depth):
    factors = arrays[0].shape[1]
    blocks = arrays[0].shape[0] // (STEPS * ROWS)
    sources = len(arrays) * blocks
    chunks = sources * ROWS // LANES
    per_chunk = LANES // ROWS
    groups = sets // NG
    wide = NG * depth
    counterparties = 2 * 128
    tile = 256

    def body(slots, lists, cur, own, *refs):
        arrs = refs[:len(arrays)]
        gd_hbm, mine, theirs, base = refs[len(arrays):len(arrays) + 4]
        sl, st, xa, xb, rates, gdv, net, gsem = refs[len(arrays) + 4:]
        gcp = pltpu.make_async_copy(gd_hbm, gdv, gsem)
        gcp.start()
        net[...] = jnp.zeros(net.shape, F32)
        for a in range(len(arrays)):
            for e in range(blocks):
                sl[slots[a * blocks + e]] = arrs[a][e * STEPS * ROWS:(e + 1) * STEPS * ROWS, :]

        def turn(ft, carry):
            f0 = pl.multiple_of(ft * tile, tile)
            for t in range(STEPS):
                for q in range(chunks):
                    blk = sl[pl.ds(per_chunk * q, per_chunk), pl.ds(t * ROWS, ROWS), pl.ds(f0, tile)]
                    o = jnp.transpose(blk.reshape(LANES, tile).astype(F32))
                    st[pl.ds(f0 * SUB + (t * chunks + q), tile, stride=SUB), :] = o
            return carry

        lax.fori_loop(0, factors // tile, turn, 0)
        for c in range(NB):
            b = st[pl.ds(c * SUB, SUB), :]
            base[pl.ds(c * SUB, SUB), :] = b
            rates[c] = jnp.exp(0.2 * b)

        def picks(j, x, k0, k1):
            for k in range(k0, k1):
                i = lists.at[pl.ds(k * groups, groups)][j]
                x[pl.ds(k * PITCH, SUB), :] = st[pl.ds(pl.multiple_of(i, SUB), SUB), :]

        sub = lax.broadcasted_iota(jnp.int32, (SUB, LANES), 0)
        halves = SUB // 2

        def value(j, x, jn, xn):
            g = gdv[j]
            loc = [jnp.zeros((SUB, LANES), F32) for _ in range(NG)]
            for p in range(halves):
                k0, k1 = wide * p // halves, wide * (p + 1) // halves
                picks(jn, xn, k0, (k0 + k1) // 2)
                xs = jnp.concatenate(
                    [x[pl.ds(2 * p, wide, stride=PITCH), :], x[pl.ds(2 * p + 1, wide, stride=PITCH), :]], axis=1
                )
                o = jnp.dot(g, xs.astype(BF16), preferred_element_type=F32)
                picks(jn, xn, (k0 + k1) // 2, k1)
                for i in range(NG):
                    for h in range(2):
                        lanes = slice(h * LANES, (h + 1) * LANES)
                        again = x[pl.ds(i * depth * PITCH + 2 * p + h, depth, stride=PITCH), :]
                        y = again * o[i * depth:(i + 1) * depth, lanes]
                        r = jnp.sum(y, axis=0, keepdims=True) + o[wide + i:wide + i + 1, lanes]
                        loc[i] = jnp.where(sub == 2 * p + h, r, loc[i])
            for i in range(NG):
                s = j * NG + i
                c = own[s]
                net[c] = net[c] + loc[i] * rates[cur[s]]

        gcp.wait()
        picks(0, xa, 0, wide)

        def loop(jj, carry):
            j = jj * 2
            value(j, xa, j + 1, xb)
            value(j + 1, xb, jnp.minimum(j + 2, groups - 1), xa)
            return carry

        lax.fori_loop(0, groups // 2, loop, 0)
        half = counterparties // 2
        theirs[...] = net[pl.ds(half, half)]
        mine[...] = net[pl.ds(0, half)]

    smem = pl.BlockSpec(memory_space=pltpu.SMEM)
    hbm = pl.BlockSpec(memory_space=pltpu.HBM)
    vmem = pl.BlockSpec(memory_space=pltpu.VMEM)
    half_shape = pltpu.VMEM((counterparties // 2, SUB, LANES), F32)
    return pl.pallas_call(
        body,
        in_specs=[smem] * 4 + [vmem] * len(arrays) + [hbm],
        out_specs=(vmem, vmem, vmem),
        out_shape=(half_shape, half_shape, pltpu.VMEM((NB * SUB, LANES), F32)),
        scratch_shapes=[
            pltpu.VMEM((sources, STEPS * ROWS, factors), BF16),
            pltpu.VMEM((factors * SUB, LANES), F32),
            pltpu.VMEM((wide * PITCH, LANES), F32),
            pltpu.VMEM((wide * PITCH, LANES), F32),
            pltpu.VMEM((NB, SUB, LANES), F32),
            pltpu.VMEM(gd.shape, BF16),
            pltpu.VMEM((counterparties, SUB, LANES), F32),
            pltpu.SemaphoreType.DMA(()),
        ],
        compiler_params=pltpu.CompilerParams(vmem_limit_bytes=40 * 1024 * 1024),
        name="revalue",
    )(
        slots, lists, currency, owner,
        *[on_chip(a) for a in arrays],
        pltpu.with_memory_space_constraint(gd, pltpu.HBM),
    )


def basis_rows(base, s):
    row = lax.broadcasted_iota(jnp.int32, (NBP - NB, LANES), 0)
    one = jnp.where(row == 0, 1.0, 0.0).astype(F32)
    return jnp.concatenate([base[pl.ds(s, NB, stride=SUB), :], one], axis=0)


def moments_of(parts, base, paths):
    chunks = SUB // STEPS

    def body(p_ref, b_ref, net_ref, out_ref):
        net_ref[...] = jnp.sum(p_ref[...], axis=0)
        pad = jnp.zeros((LANES - NBP, chunks * LANES), F32)
        m = []
        for t in range(STEPS):
            right, mine = [], []
            for q in range(chunks):
                s = t * chunks + q
                right.append(basis_rows(b_ref, s))
                mine.append(net_ref[pl.ds(s, SUB, stride=SUB), :])
            right = jnp.concatenate(right, axis=1)
            left = jnp.concatenate([right, jnp.concatenate(mine, axis=1)], axis=0)
            m.append(lax.dot_general(
                left, jnp.concatenate([right, pad], axis=0), (((1,), (1,)), ((), ())),
                precision=HIGH, preferred_element_type=F32,
            ))
        low = jnp.concatenate([
            pltpu.roll(m[t][NBP:], 2 * NBP, 1) + pltpu.roll(m[t][NB:NBP], 3 * NBP, 1) for t in range(STEPS)
        ], axis=0)
        packed = m[0][:NB] + pltpu.roll(m[1][:NB], NBP, 1) + low
        for d in range(paths):
            out_ref[d] = packed

    return pl.pallas_call(
        body,
        in_specs=[VMEM_SPEC] * 2,
        out_specs=(VMEM_SPEC, VMEM_SPEC),
        out_shape=(
            pltpu.VMEM((SUB * SUB, LANES), F32),
            pltpu.VMEM((paths, NB, LANES), F32),
        ),
        name="moments",
    )(on_chip(parts), on_chip(base))


def expose(payload, net, base, total):
    chunks = SUB // STEPS

    def body(p_ref, n_ref, b_ref, o_ref):
        acc = jnp.sum(p_ref[...], axis=0) * (1.0 / total)
        row = lax.broadcasted_iota(jnp.int32, (NBP + SUB, LANES), 0)
        lane = lax.broadcasted_iota(jnp.int32, (NBP + SUB, LANES), 1)
        diag = jnp.where((row == lane) & (row <= NB), 0.001, 0.0)
        sys = []
        for t in range(STEPS):
            rest = acc[t * SUB:(t + 1) * SUB]
            a = jnp.concatenate([
                acc if t == 0 else pltpu.roll(acc, LANES - NBP, 1),
                pltpu.roll(rest, LANES - 3 * NBP, 1),
                pltpu.roll(rest, LANES - 2 * NBP, 1),
            ], axis=0)
            sys.append(jnp.where(lane < NBP, a, 0.0) + diag)
        for k in range(NB + 1):
            for t in range(STEPS):
                a = sys[t]
                r = a[k:k + 1, :]
                c = a[:, k:k + 1] * (1.0 / a[k:k + 1, k:k + 1])
                sys[t] = jnp.where(lane == k, c, a - c * r)
        for t in range(STEPS):
            coef = sys[t][NBP:, 0:NBP]
            for q in range(chunks):
                s = t * chunks + q
                fitted = jnp.dot(coef, basis_rows(b_ref, s), precision=HIGH, preferred_element_type=F32)
                n = n_ref[pl.ds(s, SUB, stride=SUB), :]
                o_ref[t, :, q * LANES:(q + 1) * LANES] = jnp.maximum(n - 0.9 * fitted, 0.0)

    return pl.pallas_call(
        body,
        in_specs=[VMEM_SPEC] * 3,
        out_specs=VMEM_SPEC,
        out_shape=jax.ShapeDtypeStruct((STEPS, SUB, chunks * LANES), F32),
        name="expose",
    )(on_chip(payload), on_chip(net), on_chip(base))


def evolve(start_state, shocks, loading, decay):
    rows, factors = start_state.shape
    parts = 8
    deep = factors // parts

    def body(z_hbm, l_hbm, s_hbm, d_hbm, slab_ref, end_ref, z, l, s, d, sem, lsem):
        small = [
            pltpu.make_async_copy(z_hbm, z, sem.at[0]),
            pltpu.make_async_copy(s_hbm, s, sem.at[1]),
            pltpu.make_async_copy(d_hbm, d, sem.at[2]),
        ]
        large = [
            pltpu.make_async_copy(l_hbm.at[pl.ds(i * deep, deep)], l.at[pl.ds(i * deep, deep)], lsem.at[i])
            for i in range(parts)
        ]
        for cp in small[:1] + large + small[1:]:
            cp.start()
        small[0].wait()
        moved = jnp.zeros((STEPS * rows, factors), F32)
        for i in range(parts):
            large[i].wait()
            moved = moved + jnp.dot(
                z[:, i * deep:(i + 1) * deep], l[pl.ds(i * deep, deep), :], preferred_element_type=F32
            )
        for cp in small[1:]:
            cp.wait()
        first = d[...] * s[...] + moved[:rows]
        end = d[...] * first + moved[rows:]
        end_ref[...] = end
        slab_ref[...] = jnp.concatenate([first, end], axis=0).astype(BF16)

    hbm = pl.BlockSpec(memory_space=pltpu.HBM)
    vmem = pl.BlockSpec(memory_space=pltpu.VMEM)
    args = (shocks.reshape(STEPS * rows, factors), loading, start_state, decay.reshape(1, factors))
    return pl.pallas_call(
        body,
        in_specs=[hbm] * 4,
        out_specs=(vmem, vmem),
        out_shape=(
            pltpu.VMEM((STEPS * rows, factors), BF16),
            jax.ShapeDtypeStruct((rows, factors), F32),
        ),
        scratch_shapes=[
            pltpu.VMEM((STEPS * rows, factors), BF16),
            pltpu.VMEM((factors, factors), BF16),
            pltpu.VMEM((rows, factors), F32),
            pltpu.VMEM((1, factors), F32),
            pltpu.SemaphoreType.DMA((3,)),
            pltpu.SemaphoreType.DMA((parts,)),
        ],
        compiler_params=pltpu.CompilerParams(vmem_limit_bytes=24 * 1024 * 1024),
        name="evolve",
    )(*[pltpu.with_memory_space_constraint(a, pltpu.HBM) for a in args])


def per_device(start_state, shocks, loading, decay, factor_lists, delta, gamma, currency, owner):
    member = lax.axis_index("set")
    core, px, py = member % 2, (member // 2) % GRID, member // (2 * GRID)
    sets, depth = factor_lists.shape
    total = ROWS * lax.axis_size("set") * lax.axis_size("path")
    slab, state = evolve(start_state, shocks, loading, decay)

    line = [slab] + [lax.ppermute(slab, "set", hop_pairs(h, 0)) for h in HOPS[1:]]
    line = jnp.concatenate(line, axis=0)
    plane = [line] + [lax.ppermute(line, "set", hop_pairs(h, 1)) for h in HOPS[1:]]
    other = [lax.ppermute(a, "set", core_pairs()) for a in plane]

    hops = jnp.array(HOPS, jnp.int32)
    near, far = hops[None, :], hops[:, None]

    def slots_of(c):
        dx = jnp.where(c == 0, near, far)
        dy = jnp.where(c == 0, far, near)
        return (((py - dy) % GRID * GRID + (px - dx) % GRID) * 2 + c).reshape(-1)

    slots = jnp.concatenate([slots_of(core), slots_of(1 - core)]).astype(jnp.int32)
    lists = (factor_lists * SUB).reshape(sets // NG, NG * depth).T.reshape(-1)
    place = jnp.where((owner // SUB) % 2 == core, 0, 128) + owner // (2 * SUB) * SUB + owner % SUB

    gd = prepare(gamma, delta)
    mine, theirs, base = revalue(slots, lists, currency, place, plane + other, gd, sets, depth)
    mine = mine + lax.ppermute(theirs, "set", core_pairs())
    chips = [[i * 2 + c for i in range(GRID * GRID)] for c in range(2)]
    parts = lax.all_to_all(
        mine.reshape(GRID * GRID, SUB * SUB, LANES), "set", 0, 0, axis_index_groups=chips
    )
    net, payload = moments_of(parts, base, lax.axis_size("path"))
    payload = lax.all_to_all(payload, "path", 0, 0)
    return expose(payload, net, base, total), state


def solution(mesh):
    return jax.shard_map(
        per_device,
        mesh=mesh,
        in_specs=(
            P(("path", "set"), None),
            P(None, ("path", "set"), None),
            P(),
            P(),
            P("set", None),
            P("set", None),
            P("set", None, None),
            P("set"),
            P("set"),
        ),
        out_specs=(P(None, "set", "path"), P(("path", "set"), None)),
        check_vma=False,
    )
```

```python
import jax
import jax.numpy as jnp
from jax import lax
from jax.experimental import pallas as pl
from jax.experimental.pallas import tpu as pltpu
from jax.sharding import PartitionSpec as P

F32 = jnp.float32
BF16 = jnp.bfloat16
HIGH = lax.Precision.HIGHEST

NB = 16
STEPS = 2
ROWS = 16
LANES = 128
GRID = 4
HOPS = (0, 2, 1, 3)
NG = 4
PITCH = 9
SUB = 8
VMEM_SPEC = pl.BlockSpec(memory_space=pltpu.VMEM)
NBP = 24


def on_chip(a):
    return pltpu.with_memory_space_constraint(a, pltpu.VMEM)


def chip_index(y, x, core):
    return (y * GRID + x) * 2 + core


def hop_pairs(hop, flip):
    pairs = []
    for y in range(GRID):
        for x in range(GRID):
            for core in range(2):
                if core ^ flip == 0:
                    to = chip_index(y, (x + hop) % GRID, core)
                else:
                    to = chip_index((y + hop) % GRID, x, core)
                pairs.append((chip_index(y, x, core), to))
    return pairs


def core_pairs():
    return [(i, i ^ 1) for i in range(2 * GRID * GRID)]


def prepare(gamma, delta):
    sets, depth, _ = gamma.shape
    wide = NG * depth
    per = 16

    def body(g_ref, d_ref, o_ref):
        zero = jnp.zeros((depth, depth), F32)
        row = lax.broadcasted_iota(jnp.int32, (16, depth), 0)
        for b in range(per):
            for i in range(NG):
                j = b * NG + i
                g = g_ref[j].astype(F32) * 0.5
                parts = [g if k == i else zero for k in range(NG)]
                o_ref[b, i * depth:(i + 1) * depth, :] = jnp.concatenate(parts, axis=1).astype(BF16)
            d = [d_ref[b * NG + i:b * NG + i + 1, :].astype(F32) for i in range(NG)]
            tail = [jnp.where(row == i, jnp.broadcast_to(d[i], (16, depth)), 0.0) for i in range(NG)]
            o_ref[b, wide:, :] = jnp.concatenate(tail, axis=1).astype(BF16)

    return pl.pallas_call(
        body,
        grid=(sets // (NG * per),),
        in_specs=[
            pl.BlockSpec((NG * per, depth, depth), lambda i: (i, 0, 0)),
            pl.BlockSpec((NG * per, depth), lambda i: (i, 0)),
        ],
        out_specs=pl.BlockSpec((per, wide + 16, wide), lambda i: (i, 0, 0)),
        out_shape=jax.ShapeDtypeStruct((sets // NG, wide + 16, wide), BF16),
        name="prepare",
    )(gamma, delta)


def revalue(slots, lists, currency, owner, arrays, gd, end, sets, depth):
    factors = arrays[0].shape[1]
    blocks = arrays[0].shape[0] // (STEPS * ROWS)
    sources = len(arrays) * blocks
    chunks = sources * ROWS // LANES
    per_chunk = LANES // ROWS
    groups = sets // NG
    wide = NG * depth
    counterparties = 2 * 128
    tile = 256

    def body(slots, lists, cur, own, *refs):
        arrs = refs[:len(arrays)]
        gd_hbm, end_ref, mine, theirs, base, end_hbm = refs[len(arrays):len(arrays) + 6]
        sl, st, xa, xb, rates, gdv, net, gsem, esem = refs[len(arrays) + 6:]
        gcp = pltpu.make_async_copy(gd_hbm, gdv, gsem)
        gcp.start()
        ecp = pltpu.make_async_copy(end_ref, end_hbm, esem)
        ecp.start()
        net[...] = jnp.zeros(net.shape, F32)
        for a in range(len(arrays)):
            for e in range(blocks):
                sl[slots[a * blocks + e]] = arrs[a][e * STEPS * ROWS:(e + 1) * STEPS * ROWS, :]

        def turn(ft, carry):
            f0 = pl.multiple_of(ft * tile, tile)
            for t in range(STEPS):
                for q in range(chunks):
                    blk = sl[pl.ds(per_chunk * q, per_chunk), pl.ds(t * ROWS, ROWS), pl.ds(f0, tile)]
                    o = jnp.transpose(blk.reshape(LANES, tile).astype(F32))
                    st[pl.ds(f0 * PITCH + (t * chunks + q), tile, stride=PITCH), :] = o
            return carry

        lax.fori_loop(0, factors // tile, turn, 0)
        for c in range(NB):
            b = st[pl.ds(c * PITCH, SUB), :]
            base[pl.ds(c * SUB, SUB), :] = b
            rates[c] = jnp.exp(0.2 * b)

        def picks(j, x, k0, k1):
            for k in range(k0, k1):
                i = lists.at[pl.ds(k * groups, groups)][j]
                x[pl.ds(k * PITCH, SUB), :] = st[pl.ds(i, SUB), :]

        sub = lax.broadcasted_iota(jnp.int32, (SUB, LANES), 0)
        halves = SUB // 2

        def value(j, x, jn, xn):
            g = gdv[j]
            loc = [jnp.zeros((SUB, LANES), F32) for _ in range(NG)]
            for p in range(halves):
                k0, k1 = wide * p // halves, wide * (p + 1) // halves
                picks(jn, xn, k0, (k0 + k1) // 2)
                xs = jnp.concatenate(
                    [x[pl.ds(2 * p, wide, stride=PITCH), :], x[pl.ds(2 * p + 1, wide, stride=PITCH), :]], axis=1
                )
                o = jnp.dot(g, xs.astype(BF16), preferred_element_type=F32)
                picks(jn, xn, (k0 + k1) // 2, k1)
                for i in range(NG):
                    for h in range(2):
                        lanes = slice(h * LANES, (h + 1) * LANES)
                        again = x[pl.ds(i * depth * PITCH + 2 * p + h, depth, stride=PITCH), :]
                        y = again * o[i * depth:(i + 1) * depth, lanes]
                        r = jnp.sum(y, axis=0, keepdims=True) + o[wide + i:wide + i + 1, lanes]
                        loc[i] = jnp.where(sub == 2 * p + h, r, loc[i])
            for i in range(NG):
                s = j * NG + i
                c = own[s]
                net[c] = net[c] + loc[i] * rates[cur[s]]

        gcp.wait()
        picks(0, xa, 0, wide)

        def loop(jj, carry):
            j = jj * 2
            value(j, xa, j + 1, xb)
            value(j + 1, xb, jnp.minimum(j + 2, groups - 1), xa)
            return carry

        lax.fori_loop(0, groups // 2, loop, 0)
        half = counterparties // 2
        theirs[...] = net[pl.ds(half, half)]
        mine[...] = net[pl.ds(0, half)]
        ecp.wait()

    smem = pl.BlockSpec(memory_space=pltpu.SMEM)
    hbm = pl.BlockSpec(memory_space=pltpu.HBM)
    vmem = pl.BlockSpec(memory_space=pltpu.VMEM)
    half_shape = pltpu.VMEM((counterparties // 2, SUB, LANES), F32)
    return pl.pallas_call(
        body,
        in_specs=[smem] * 4 + [vmem] * len(arrays) + [hbm, vmem],
        out_specs=(vmem, vmem, vmem, hbm),
        out_shape=(
            half_shape, half_shape, pltpu.VMEM((NB * SUB, LANES), F32), jax.ShapeDtypeStruct(end.shape, F32),
        ),
        scratch_shapes=[
            pltpu.VMEM((sources, STEPS * ROWS, factors), BF16),
            pltpu.VMEM((factors * PITCH, LANES), F32),
            pltpu.VMEM((wide * PITCH, LANES), F32),
            pltpu.VMEM((wide * PITCH, LANES), F32),
            pltpu.VMEM((NB, SUB, LANES), F32),
            pltpu.VMEM(gd.shape, BF16),
            pltpu.VMEM((counterparties, SUB, LANES), F32),
            pltpu.SemaphoreType.DMA(()),
            pltpu.SemaphoreType.DMA(()),
        ],
        compiler_params=pltpu.CompilerParams(vmem_limit_bytes=40 * 1024 * 1024),
        name="revalue",
    )(
        slots, lists, currency, owner,
        *[on_chip(a) for a in arrays],
        pltpu.with_memory_space_constraint(gd, pltpu.HBM),
        on_chip(end),
    )


def basis_rows(base, s):
    row = lax.broadcasted_iota(jnp.int32, (NBP - NB, LANES), 0)
    one = jnp.where(row == 0, 1.0, 0.0).astype(F32)
    return jnp.concatenate([base[pl.ds(s, NB, stride=SUB), :], one], axis=0)


def moments_of(parts, base, paths):
    chunks = SUB // STEPS

    def body(p_ref, b_ref, net_ref, out_ref):
        net_ref[...] = jnp.sum(p_ref[...], axis=0)
        pad = jnp.zeros((LANES - NBP, chunks * LANES), F32)
        m = []
        for t in range(STEPS):
            right, mine = [], []
            for q in range(chunks):
                s = t * chunks + q
                right.append(basis_rows(b_ref, s))
                mine.append(net_ref[pl.ds(s, SUB, stride=SUB), :])
            right = jnp.concatenate(right, axis=1)
            left = jnp.concatenate([right, jnp.concatenate(mine, axis=1)], axis=0)
            m.append(lax.dot_general(
                left, jnp.concatenate([right, pad], axis=0), (((1,), (1,)), ((), ())),
                precision=HIGH, preferred_element_type=F32,
            ))
        low = jnp.concatenate([
            pltpu.roll(m[t][NBP:], 2 * NBP, 1) + pltpu.roll(m[t][NB:NBP], 3 * NBP, 1) for t in range(STEPS)
        ], axis=0)
        packed = m[0][:NB] + pltpu.roll(m[1][:NB], NBP, 1) + low
        for d in range(paths):
            out_ref[d] = packed

    return pl.pallas_call(
        body,
        in_specs=[VMEM_SPEC] * 2,
        out_specs=(VMEM_SPEC, VMEM_SPEC),
        out_shape=(
            pltpu.VMEM((SUB * SUB, LANES), F32),
            pltpu.VMEM((paths, NB, LANES), F32),
        ),
        name="moments",
    )(on_chip(parts), on_chip(base))


def expose(payload, net, base, total):
    chunks = SUB // STEPS

    def body(p_ref, n_ref, b_ref, o_hbm, o_ref, sem):
        acc = jnp.sum(p_ref[...], axis=0) * (1.0 / total)
        row = lax.broadcasted_iota(jnp.int32, (NBP + SUB, LANES), 0)
        lane = lax.broadcasted_iota(jnp.int32, (NBP + SUB, LANES), 1)
        diag = jnp.where((row == lane) & (row <= NB), 0.001, 0.0)
        sys = []
        for t in range(STEPS):
            rest = acc[t * SUB:(t + 1) * SUB]
            a = jnp.concatenate([
                acc if t == 0 else pltpu.roll(acc, LANES - NBP, 1),
                pltpu.roll(rest, LANES - 3 * NBP, 1),
                pltpu.roll(rest, LANES - 2 * NBP, 1),
            ], axis=0)
            sys.append(jnp.where(lane < NBP, a, 0.0) + diag)
        for k in range(NB + 1):
            for t in range(STEPS):
                a = sys[t]
                r = a[k:k + 1, :]
                c = a[:, k:k + 1] * (1.0 / a[k:k + 1, k:k + 1])
                sys[t] = jnp.where(lane == k, c, a - c * r)
        for t in range(STEPS):
            coef = sys[t][NBP:, 0:NBP]
            steps = [t * chunks + q for q in range(chunks)]
            fitted = jnp.dot(
                coef, jnp.concatenate([basis_rows(b_ref, s) for s in steps], axis=1),
                precision=HIGH, preferred_element_type=F32,
            )
            n = jnp.concatenate([n_ref[pl.ds(s, SUB, stride=SUB), :] for s in steps], axis=1)
            o_ref[t] = jnp.maximum(n - 0.9 * fitted, 0.0)
        cp = pltpu.make_async_copy(o_ref, o_hbm, sem)
        cp.start()
        cp.wait()

    return pl.pallas_call(
        body,
        in_specs=[VMEM_SPEC] * 3,
        out_specs=pl.BlockSpec(memory_space=pltpu.HBM),
        out_shape=jax.ShapeDtypeStruct((STEPS, SUB, chunks * LANES), F32),
        scratch_shapes=[pltpu.VMEM((STEPS, SUB, chunks * LANES), F32), pltpu.SemaphoreType.DMA(())],
        name="expose",
    )(on_chip(payload), on_chip(net), on_chip(base))


def evolve(start_state, shocks, loading, decay):
    rows, factors = start_state.shape
    parts = 8
    deep = factors // parts

    def body(z_hbm, l_hbm, s_hbm, d_hbm, slab_ref, end_ref, z, l, s, d, sem, lsem):
        small = [
            pltpu.make_async_copy(z_hbm, z, sem.at[0]),
            pltpu.make_async_copy(s_hbm, s, sem.at[1]),
            pltpu.make_async_copy(d_hbm, d, sem.at[2]),
        ]
        large = [
            pltpu.make_async_copy(l_hbm.at[pl.ds(i * deep, deep)], l.at[pl.ds(i * deep, deep)], lsem.at[i])
            for i in range(parts)
        ]
        for cp in small[:1] + large + small[1:]:
            cp.start()
        small[0].wait()
        moved = jnp.zeros((STEPS * rows, factors), F32)
        for i in range(parts):
            large[i].wait()
            moved = moved + jnp.dot(
                z[:, i * deep:(i + 1) * deep], l[pl.ds(i * deep, deep), :], preferred_element_type=F32
            )
        for cp in small[1:]:
            cp.wait()
        first = d[...] * s[...] + moved[:rows]
        end = d[...] * first + moved[rows:]
        end_ref[...] = end
        slab_ref[...] = jnp.concatenate([first, end], axis=0).astype(BF16)

    hbm = pl.BlockSpec(memory_space=pltpu.HBM)
    vmem = pl.BlockSpec(memory_space=pltpu.VMEM)
    args = (shocks.reshape(STEPS * rows, factors), loading, start_state, decay.reshape(1, factors))
    return pl.pallas_call(
        body,
        in_specs=[hbm] * 4,
        out_specs=(vmem, vmem),
        out_shape=(
            pltpu.VMEM((STEPS * rows, factors), BF16),
            pltpu.VMEM((rows, factors), F32),
        ),
        scratch_shapes=[
            pltpu.VMEM((STEPS * rows, factors), BF16),
            pltpu.VMEM((factors, factors), BF16),
            pltpu.VMEM((rows, factors), F32),
            pltpu.VMEM((1, factors), F32),
            pltpu.SemaphoreType.DMA((3,)),
            pltpu.SemaphoreType.DMA((parts,)),
        ],
        compiler_params=pltpu.CompilerParams(vmem_limit_bytes=24 * 1024 * 1024),
        name="evolve",
    )(*[pltpu.with_memory_space_constraint(a, pltpu.HBM) for a in args])


def per_device(start_state, shocks, loading, decay, factor_lists, delta, gamma, currency, owner):
    member = lax.axis_index("set")
    core, px, py = member % 2, (member // 2) % GRID, member // (2 * GRID)
    sets, depth = factor_lists.shape
    total = ROWS * lax.axis_size("set") * lax.axis_size("path")
    slab, state = evolve(start_state, shocks, loading, decay)

    line = [slab] + [lax.ppermute(slab, "set", hop_pairs(h, 0)) for h in HOPS[1:]]
    line = jnp.concatenate(line, axis=0)
    plane = [line] + [lax.ppermute(line, "set", hop_pairs(h, 1)) for h in HOPS[1:]]
    other = [lax.ppermute(a, "set", core_pairs()) for a in plane]

    hops = jnp.array(HOPS, jnp.int32)
    near, far = hops[None, :], hops[:, None]

    def slots_of(c):
        dx = jnp.where(c == 0, near, far)
        dy = jnp.where(c == 0, far, near)
        return (((py - dy) % GRID * GRID + (px - dx) % GRID) * 2 + c).reshape(-1)

    slots = jnp.concatenate([slots_of(core), slots_of(1 - core)]).astype(jnp.int32)
    lists = (factor_lists * PITCH).reshape(sets // NG, NG * depth).T.reshape(-1)
    place = jnp.where((owner // SUB) % 2 == core, 0, 128) + owner // (2 * SUB) * SUB + owner % SUB

    gd = prepare(gamma, delta)
    mine, theirs, base, state = revalue(
        slots, lists, currency, place, plane + other, gd, state, sets, depth
    )
    mine = mine + lax.ppermute(theirs, "set", core_pairs())
    chips = [[i * 2 + c for i in range(GRID * GRID)] for c in range(2)]
    parts = lax.all_to_all(
        mine.reshape(GRID * GRID, SUB * SUB, LANES), "set", 0, 0, axis_index_groups=chips
    )
    net, payload = moments_of(parts, base, lax.axis_size("path"))
    payload = lax.all_to_all(payload, "path", 0, 0)
    return expose(payload, net, base, total), state


def solution(mesh):
    return jax.shard_map(
        per_device,
        mesh=mesh,
        in_specs=(
            P(("path", "set"), None),
            P(None, ("path", "set"), None),
            P(),
            P(),
            P("set", None),
            P("set", None),
            P("set", None, None),
            P("set"),
            P("set"),
        ),
        out_specs=(P(None, "set", "path"), P(("path", "set"), None)),
        check_vma=False,
    )
```

```python
import jax
import jax.numpy as jnp
from jax import lax
from jax.experimental import pallas as pl
from jax.experimental.pallas import tpu as pltpu
from jax.sharding import PartitionSpec as P

F32 = jnp.float32
BF16 = jnp.bfloat16
HIGH = lax.Precision.HIGHEST

NB = 16
STEPS = 2
ROWS = 16
LANES = 128
GRID = 4
HOPS = (0, 2, 3, 1)
NG = 4
PITCH = 9
SUB = 8
VMEM_SPEC = pl.BlockSpec(memory_space=pltpu.VMEM)
NBP = 24


def on_chip(a):
    return pltpu.with_memory_space_constraint(a, pltpu.VMEM)


def chip_index(y, x, core):
    return (y * GRID + x) * 2 + core


def hop_pairs(hop, flip):
    pairs = []
    for y in range(GRID):
        for x in range(GRID):
            for core in range(2):
                if core ^ flip == 0:
                    to = chip_index(y, (x + hop) % GRID, core)
                else:
                    to = chip_index((y + hop) % GRID, x, core)
                pairs.append((chip_index(y, x, core), to))
    return pairs


def core_pairs():
    return [(i, i ^ 1) for i in range(2 * GRID * GRID)]


def prepare(gamma, delta):
    sets, depth, _ = gamma.shape
    wide = NG * depth
    per = 16

    def body(g_ref, d_ref, o_ref):
        zero = jnp.zeros((depth, depth), F32)
        row = lax.broadcasted_iota(jnp.int32, (16, depth), 0)
        for b in range(per):
            for i in range(NG):
                j = b * NG + i
                g = g_ref[j].astype(F32) * 0.5
                parts = [g if k == i else zero for k in range(NG)]
                o_ref[b, i * depth:(i + 1) * depth, :] = jnp.concatenate(parts, axis=1).astype(BF16)
            d = [d_ref[b * NG + i:b * NG + i + 1, :].astype(F32) for i in range(NG)]
            tail = [jnp.where(row == i, jnp.broadcast_to(d[i], (16, depth)), 0.0) for i in range(NG)]
            o_ref[b, wide:, :] = jnp.concatenate(tail, axis=1).astype(BF16)

    return pl.pallas_call(
        body,
        grid=(sets // (NG * per),),
        in_specs=[
            pl.BlockSpec((NG * per, depth, depth), lambda i: (i, 0, 0)),
            pl.BlockSpec((NG * per, depth), lambda i: (i, 0)),
        ],
        out_specs=pl.BlockSpec((per, wide + 16, wide), lambda i: (i, 0, 0)),
        out_shape=jax.ShapeDtypeStruct((sets // NG, wide + 16, wide), BF16),
        name="prepare",
    )(gamma, delta)


def revalue(slots, lists, currency, owner, arrays, gd, end, sets, depth):
    factors = arrays[0].shape[1]
    blocks = arrays[0].shape[0] // (STEPS * ROWS)
    sources = len(arrays) * blocks
    chunks = sources * ROWS // LANES
    per_chunk = LANES // ROWS
    groups = sets // NG
    wide = NG * depth
    counterparties = 2 * 128
    tile = 256

    def body(slots, lists, cur, own, *refs):
        arrs = refs[:len(arrays)]
        gd_hbm, end_ref, mine, theirs, base, end_hbm = refs[len(arrays):len(arrays) + 6]
        sl, st, xa, xb, rates, gdv, net, gsem, esem = refs[len(arrays) + 6:]
        gcp = pltpu.make_async_copy(gd_hbm, gdv, gsem)
        gcp.start()
        ecp = pltpu.make_async_copy(end_ref, end_hbm, esem)
        ecp.start()
        net[...] = jnp.zeros(net.shape, F32)
        for a in range(len(arrays)):
            for e in range(blocks):
                sl[slots[a * blocks + e]] = arrs[a][e * STEPS * ROWS:(e + 1) * STEPS * ROWS, :]

        def turn(ft, carry):
            f0 = pl.multiple_of(ft * tile, tile)
            for t in range(STEPS):
                for q in range(chunks):
                    blk = sl[pl.ds(per_chunk * q, per_chunk), pl.ds(t * ROWS, ROWS), pl.ds(f0, tile)]
                    o = jnp.transpose(blk.reshape(LANES, tile).astype(F32))
                    st[pl.ds(f0 * PITCH + (t * chunks + q), tile, stride=PITCH), :] = o
            return carry

        lax.fori_loop(0, factors // tile, turn, 0)
        for c in range(NB):
            b = st[pl.ds(c * PITCH, SUB), :]
            base[pl.ds(c * SUB, SUB), :] = b
            rates[c] = jnp.exp(0.2 * b)

        def picks(j, x, k0, k1):
            for k in range(k0, k1):
                i = lists.at[pl.ds(k * groups, groups)][j]
                x[pl.ds(k * PITCH, SUB), :] = st[pl.ds(i, SUB), :]

        sub = lax.broadcasted_iota(jnp.int32, (SUB, LANES), 0)
        halves = SUB // 2

        def value(j, x, jn, xn):
            g = gdv[j]
            loc = [jnp.zeros((SUB, LANES), F32) for _ in range(NG)]
            for p in range(halves):
                k0, k1 = wide * p // halves, wide * (p + 1) // halves
                picks(jn, xn, k0, (k0 + k1) // 2)
                xs = jnp.concatenate(
                    [x[pl.ds(2 * p, wide, stride=PITCH), :], x[pl.ds(2 * p + 1, wide, stride=PITCH), :]], axis=1
                )
                o = jnp.dot(g, xs.astype(BF16), preferred_element_type=F32)
                picks(jn, xn, (k0 + k1) // 2, k1)
                for i in range(NG):
                    for h in range(2):
                        lanes = slice(h * LANES, (h + 1) * LANES)
                        again = x[pl.ds(i * depth * PITCH + 2 * p + h, depth, stride=PITCH), :]
                        y = again * o[i * depth:(i + 1) * depth, lanes]
                        r = jnp.sum(y, axis=0, keepdims=True) + o[wide + i:wide + i + 1, lanes]
                        loc[i] = jnp.where(sub == 2 * p + h, r, loc[i])
            for i in range(NG):
                s = j * NG + i
                c = own[s]
                net[c] = net[c] + loc[i] * rates[cur[s]]

        gcp.wait()
        picks(0, xa, 0, wide)

        def loop(jj, carry):
            j = jj * 2
            value(j, xa, j + 1, xb)
            value(j + 1, xb, jnp.minimum(j + 2, groups - 1), xa)
            return carry

        lax.fori_loop(0, groups // 2, loop, 0)
        half = counterparties // 2
        theirs[...] = net[pl.ds(half, half)]
        mine[...] = net[pl.ds(0, half)]
        ecp.wait()

    smem = pl.BlockSpec(memory_space=pltpu.SMEM)
    hbm = pl.BlockSpec(memory_space=pltpu.HBM)
    vmem = pl.BlockSpec(memory_space=pltpu.VMEM)
    half_shape = pltpu.VMEM((counterparties // 2, SUB, LANES), F32)
    return pl.pallas_call(
        body,
        in_specs=[smem] * 4 + [vmem] * len(arrays) + [hbm, vmem],
        out_specs=(vmem, vmem, vmem, hbm),
        out_shape=(
            half_shape, half_shape, pltpu.VMEM((NB * SUB, LANES), F32), jax.ShapeDtypeStruct(end.shape, F32),
        ),
        scratch_shapes=[
            pltpu.VMEM((sources, STEPS * ROWS, factors), BF16),
            pltpu.VMEM((factors * PITCH, LANES), F32),
            pltpu.VMEM((wide * PITCH, LANES), F32),
            pltpu.VMEM((wide * PITCH, LANES), F32),
            pltpu.VMEM((NB, SUB, LANES), F32),
            pltpu.VMEM(gd.shape, BF16),
            pltpu.VMEM((counterparties, SUB, LANES), F32),
            pltpu.SemaphoreType.DMA(()),
            pltpu.SemaphoreType.DMA(()),
        ],
        compiler_params=pltpu.CompilerParams(vmem_limit_bytes=40 * 1024 * 1024),
        name="revalue",
    )(
        slots, lists, currency, owner,
        *[on_chip(a) for a in arrays],
        pltpu.with_memory_space_constraint(gd, pltpu.HBM),
        on_chip(end),
    )


def basis_rows(base, s):
    row = lax.broadcasted_iota(jnp.int32, (NBP - NB, LANES), 0)
    one = jnp.where(row == 0, 1.0, 0.0).astype(F32)
    return jnp.concatenate([base[pl.ds(s, NB, stride=SUB), :], one], axis=0)


def moments_of(parts, base, paths):
    chunks = SUB // STEPS

    def body(p_ref, b_ref, net_ref, out_ref):
        net_ref[...] = jnp.sum(p_ref[...], axis=0)
        pad = jnp.zeros((LANES - NBP, chunks * LANES), F32)
        m = []
        for t in range(STEPS):
            right, mine = [], []
            for q in range(chunks):
                s = t * chunks + q
                right.append(basis_rows(b_ref, s))
                mine.append(net_ref[pl.ds(s, SUB, stride=SUB), :])
            right = jnp.concatenate(right, axis=1)
            left = jnp.concatenate([right, jnp.concatenate(mine, axis=1)], axis=0)
            m.append(lax.dot_general(
                left, jnp.concatenate([right, pad], axis=0), (((1,), (1,)), ((), ())),
                precision=HIGH, preferred_element_type=F32,
            ))
        low = jnp.concatenate([
            pltpu.roll(m[t][NBP:], 2 * NBP, 1) + pltpu.roll(m[t][NB:NBP], 3 * NBP, 1) for t in range(STEPS)
        ], axis=0)
        packed = m[0][:NB] + pltpu.roll(m[1][:NB], NBP, 1) + low
        for d in range(paths):
            out_ref[d] = packed

    return pl.pallas_call(
        body,
        in_specs=[VMEM_SPEC] * 2,
        out_specs=(VMEM_SPEC, VMEM_SPEC),
        out_shape=(
            pltpu.VMEM((SUB * SUB, LANES), F32),
            pltpu.VMEM((paths, NB, LANES), F32),
        ),
        name="moments",
    )(on_chip(parts), on_chip(base))


def expose(payload, net, base, total):
    chunks = SUB // STEPS

    def body(p_ref, n_ref, b_ref, o_hbm, o_ref, sem):
        acc = jnp.sum(p_ref[...], axis=0) * (1.0 / total)
        row = lax.broadcasted_iota(jnp.int32, (NBP + SUB, LANES), 0)
        lane = lax.broadcasted_iota(jnp.int32, (NBP + SUB, LANES), 1)
        diag = jnp.where((row == lane) & (row <= NB), 0.001, 0.0)
        sys = []
        for t in range(STEPS):
            rest = acc[t * SUB:(t + 1) * SUB]
            a = jnp.concatenate([
                acc if t == 0 else pltpu.roll(acc, LANES - NBP, 1),
                pltpu.roll(rest, LANES - 3 * NBP, 1),
                pltpu.roll(rest, LANES - 2 * NBP, 1),
            ], axis=0)
            sys.append(jnp.where(lane < NBP, a, 0.0) + diag)
        for k in range(NB + 1):
            for t in range(STEPS):
                a = sys[t]
                r = a[k:k + 1, :]
                c = a[:, k:k + 1] * (1.0 / a[k:k + 1, k:k + 1])
                sys[t] = jnp.where(lane == k, c, a - c * r)
        for t in range(STEPS):
            coef = sys[t][NBP:, 0:NBP]
            steps = [t * chunks + q for q in range(chunks)]
            fitted = jnp.dot(
                coef, jnp.concatenate([basis_rows(b_ref, s) for s in steps], axis=1),
                precision=HIGH, preferred_element_type=F32,
            )
            n = jnp.concatenate([n_ref[pl.ds(s, SUB, stride=SUB), :] for s in steps], axis=1)
            o_ref[t] = jnp.maximum(n - 0.9 * fitted, 0.0)
        cp = pltpu.make_async_copy(o_ref, o_hbm, sem)
        cp.start()
        cp.wait()

    return pl.pallas_call(
        body,
        in_specs=[VMEM_SPEC] * 3,
        out_specs=pl.BlockSpec(memory_space=pltpu.HBM),
        out_shape=jax.ShapeDtypeStruct((STEPS, SUB, chunks * LANES), F32),
        scratch_shapes=[pltpu.VMEM((STEPS, SUB, chunks * LANES), F32), pltpu.SemaphoreType.DMA(())],
        name="expose",
    )(on_chip(payload), on_chip(net), on_chip(base))


def evolve(start_state, shocks, loading, decay):
    rows, factors = start_state.shape
    parts = 8
    deep = factors // parts

    def body(z_hbm, l_hbm, s_hbm, d_hbm, slab_ref, end_ref, z, l, s, d, sem, lsem):
        small = [
            pltpu.make_async_copy(z_hbm, z, sem.at[0]),
            pltpu.make_async_copy(s_hbm, s, sem.at[1]),
            pltpu.make_async_copy(d_hbm, d, sem.at[2]),
        ]
        large = [
            pltpu.make_async_copy(l_hbm.at[pl.ds(i * deep, deep)], l.at[pl.ds(i * deep, deep)], lsem.at[i])
            for i in range(parts)
        ]
        for cp in small[:1] + large + small[1:]:
            cp.start()
        small[0].wait()
        moved = jnp.zeros((STEPS * rows, factors), F32)
        for i in range(parts):
            large[i].wait()
            moved = moved + jnp.dot(
                z[:, i * deep:(i + 1) * deep], l[pl.ds(i * deep, deep), :], preferred_element_type=F32
            )
        for cp in small[1:]:
            cp.wait()
        first = d[...] * s[...] + moved[:rows]
        end = d[...] * first + moved[rows:]
        end_ref[...] = end
        slab_ref[...] = jnp.concatenate([first, end], axis=0).astype(BF16)

    hbm = pl.BlockSpec(memory_space=pltpu.HBM)
    vmem = pl.BlockSpec(memory_space=pltpu.VMEM)
    args = (shocks.reshape(STEPS * rows, factors), loading, start_state, decay.reshape(1, factors))
    return pl.pallas_call(
        body,
        in_specs=[hbm] * 4,
        out_specs=(vmem, vmem),
        out_shape=(
            pltpu.VMEM((STEPS * rows, factors), BF16),
            pltpu.VMEM((rows, factors), F32),
        ),
        scratch_shapes=[
            pltpu.VMEM((STEPS * rows, factors), BF16),
            pltpu.VMEM((factors, factors), BF16),
            pltpu.VMEM((rows, factors), F32),
            pltpu.VMEM((1, factors), F32),
            pltpu.SemaphoreType.DMA((3,)),
            pltpu.SemaphoreType.DMA((parts,)),
        ],
        compiler_params=pltpu.CompilerParams(vmem_limit_bytes=24 * 1024 * 1024),
        name="evolve",
    )(*[pltpu.with_memory_space_constraint(a, pltpu.HBM) for a in args])


def per_device(start_state, shocks, loading, decay, factor_lists, delta, gamma, currency, owner):
    member = lax.axis_index("set")
    core, px, py = member % 2, (member // 2) % GRID, member // (2 * GRID)
    sets, depth = factor_lists.shape
    total = ROWS * lax.axis_size("set") * lax.axis_size("path")
    slab, state = evolve(start_state, shocks, loading, decay)

    line = [slab] + [lax.ppermute(slab, "set", hop_pairs(h, 0)) for h in HOPS[1:]]
    line = jnp.concatenate(line, axis=0)
    plane = [line] + [lax.ppermute(line, "set", hop_pairs(h, 1)) for h in HOPS[1:]]
    other = [lax.ppermute(a, "set", core_pairs()) for a in plane]

    hops = jnp.array(HOPS, jnp.int32)
    near, far = hops[None, :], hops[:, None]

    def slots_of(c):
        dx = jnp.where(c == 0, near, far)
        dy = jnp.where(c == 0, far, near)
        return (((py - dy) % GRID * GRID + (px - dx) % GRID) * 2 + c).reshape(-1)

    slots = jnp.concatenate([slots_of(core), slots_of(1 - core)]).astype(jnp.int32)
    lists = (factor_lists * PITCH).reshape(sets // NG, NG * depth).T.reshape(-1)
    place = jnp.where((owner // SUB) % 2 == core, 0, 128) + owner // (2 * SUB) * SUB + owner % SUB

    gd = prepare(gamma, delta)
    mine, theirs, base, state = revalue(
        slots, lists, currency, place, plane + other, gd, state, sets, depth
    )
    mine = mine + lax.ppermute(theirs, "set", core_pairs())
    chips = [[i * 2 + c for i in range(GRID * GRID)] for c in range(2)]
    parts = lax.all_to_all(
        mine.reshape(GRID * GRID, SUB * SUB, LANES), "set", 0, 0, axis_index_groups=chips
    )
    net, payload = moments_of(parts, base, lax.axis_size("path"))
    payload = lax.all_to_all(payload, "path", 0, 0)
    return expose(payload, net, base, total), state


def solution(mesh):
    return jax.shard_map(
        per_device,
        mesh=mesh,
        in_specs=(
            P(("path", "set"), None),
            P(None, ("path", "set"), None),
            P(),
            P(),
            P("set", None),
            P("set", None),
            P("set", None, None),
            P("set"),
            P("set"),
        ),
        out_specs=(P(None, "set", "path"), P(("path", "set"), None)),
        check_vma=False,
    )
```

```python
import jax
import jax.numpy as jnp
from jax import lax
from jax.experimental import pallas as pl
from jax.experimental.pallas import tpu as pltpu
from jax.sharding import PartitionSpec as P

F32 = jnp.float32
BF16 = jnp.bfloat16
HIGH = lax.Precision.HIGHEST

NB = 16
STEPS = 2
ROWS = 16
LANES = 128
GRID = 4
HOPS = (0, 2, 3, 1)
NG = 4
PITCH = 9
SUB = 8
VMEM_SPEC = pl.BlockSpec(memory_space=pltpu.VMEM)
NBP = 24


def on_chip(a):
    return pltpu.with_memory_space_constraint(a, pltpu.VMEM)


def chip_index(y, x, core):
    return (y * GRID + x) * 2 + core


def hop_pairs(hop, flip):
    pairs = []
    for y in range(GRID):
        for x in range(GRID):
            for core in range(2):
                if core ^ flip == 0:
                    to = chip_index(y, (x + hop) % GRID, core)
                else:
                    to = chip_index((y + hop) % GRID, x, core)
                pairs.append((chip_index(y, x, core), to))
    return pairs


def core_pairs():
    return [(i, i ^ 1) for i in range(2 * GRID * GRID)]


def prepare(gamma, delta):
    sets, depth, _ = gamma.shape
    wide = NG * depth
    per = 16

    def body(g_ref, d_ref, o_ref):
        zero = jnp.zeros((depth, depth), F32)
        row = lax.broadcasted_iota(jnp.int32, (16, depth), 0)
        for b in range(per):
            for i in range(NG):
                j = b * NG + i
                g = g_ref[j].astype(F32) * 0.5
                parts = [g if k == i else zero for k in range(NG)]
                o_ref[b, i * depth:(i + 1) * depth, :] = jnp.concatenate(parts, axis=1).astype(BF16)
            d = [d_ref[b * NG + i:b * NG + i + 1, :].astype(F32) for i in range(NG)]
            tail = [jnp.where(row == i, jnp.broadcast_to(d[i], (16, depth)), 0.0) for i in range(NG)]
            o_ref[b, wide:, :] = jnp.concatenate(tail, axis=1).astype(BF16)

    return pl.pallas_call(
        body,
        grid=(sets // (NG * per),),
        in_specs=[
            pl.BlockSpec((NG * per, depth, depth), lambda i: (i, 0, 0)),
            pl.BlockSpec((NG * per, depth), lambda i: (i, 0)),
        ],
        out_specs=pl.BlockSpec((per, wide + 16, wide), lambda i: (i, 0, 0)),
        out_shape=jax.ShapeDtypeStruct((sets // NG, wide + 16, wide), BF16),
        name="prepare",
    )(gamma, delta)


def revalue(slots, lists, currency, owner, arrays, gd, end, sets, depth):
    factors = arrays[0].shape[1]
    blocks = arrays[0].shape[0] // (STEPS * ROWS)
    sources = len(arrays) * blocks
    chunks = sources * ROWS // LANES
    per_chunk = LANES // ROWS
    groups = sets // NG
    wide = NG * depth
    counterparties = 2 * 128
    tile = 256

    def body(slots, lists, cur, own, *refs):
        arrs = refs[:len(arrays)]
        gd_hbm, end_ref, mine, theirs, base, end_hbm = refs[len(arrays):len(arrays) + 6]
        sl, st, xa, xb, rates, gdv, net, gsem, esem = refs[len(arrays) + 6:]
        gcp = pltpu.make_async_copy(gd_hbm, gdv, gsem)
        gcp.start()
        ecp = pltpu.make_async_copy(end_ref, end_hbm, esem)
        ecp.start()
        net[...] = jnp.zeros(net.shape, F32)
        for a in range(len(arrays)):
            for e in range(blocks):
                sl[slots[a * blocks + e]] = arrs[a][e * STEPS * ROWS:(e + 1) * STEPS * ROWS, :]

        def turn(ft, carry):
            f0 = pl.multiple_of(ft * tile, tile)
            for t in range(STEPS):
                for q in range(chunks):
                    blk = sl[pl.ds(per_chunk * q, per_chunk), pl.ds(t * ROWS, ROWS), pl.ds(f0, tile)]
                    o = jnp.transpose(blk.reshape(LANES, tile).astype(F32))
                    st[pl.ds(f0 * PITCH + (t * chunks + q), tile, stride=PITCH), :] = o
            return carry

        lax.fori_loop(0, factors // tile, turn, 0)
        for c in range(NB):
            b = st[pl.ds(c * PITCH, SUB), :]
            base[pl.ds(c * SUB, SUB), :] = b
            rates[c] = jnp.exp(0.2 * b)

        def picks(j, x, k0, k1):
            for k in range(k0, k1):
                i = lists.at[pl.ds(k * groups, groups)][j]
                x[pl.ds(k * PITCH, SUB), :] = st[pl.ds(i, SUB), :]

        sub = lax.broadcasted_iota(jnp.int32, (SUB, LANES), 0)
        halves = SUB // 2

        def value(j, x, jn, xn):
            g = gdv[j]
            loc = [jnp.zeros((SUB, LANES), F32) for _ in range(NG)]
            for p in range(halves):
                k0, k1 = wide * p // halves, wide * (p + 1) // halves
                picks(jn, xn, k0, (k0 + k1) // 2)
                xs = jnp.concatenate(
                    [x[pl.ds(2 * p, wide, stride=PITCH), :], x[pl.ds(2 * p + 1, wide, stride=PITCH), :]], axis=1
                )
                o = jnp.dot(g, xs.astype(BF16), preferred_element_type=F32)
                picks(jn, xn, (k0 + k1) // 2, k1)
                for i in range(NG):
                    for h in range(2):
                        lanes = slice(h * LANES, (h + 1) * LANES)
                        again = x[pl.ds(i * depth * PITCH + 2 * p + h, depth, stride=PITCH), :]
                        y = again * o[i * depth:(i + 1) * depth, lanes]
                        r = jnp.sum(y, axis=0, keepdims=True) + o[wide + i:wide + i + 1, lanes]
                        loc[i] = jnp.where(sub == 2 * p + h, r, loc[i])
            for i in range(NG):
                s = j * NG + i
                c = own[s]
                net[c] = net[c] + loc[i] * rates[cur[s]]

        gcp.wait()
        picks(0, xa, 0, wide)

        def loop(jj, carry):
            j = jj * 2
            value(j, xa, j + 1, xb)
            value(j + 1, xb, jnp.minimum(j + 2, groups - 1), xa)
            return carry

        lax.fori_loop(0, groups // 2, loop, 0)
        half = counterparties // 2
        theirs[...] = net[pl.ds(half, half)]
        mine[...] = net[pl.ds(0, half)]
        ecp.wait()

    smem = pl.BlockSpec(memory_space=pltpu.SMEM)
    hbm = pl.BlockSpec(memory_space=pltpu.HBM)
    vmem = pl.BlockSpec(memory_space=pltpu.VMEM)
    half_shape = pltpu.VMEM((counterparties // 2, SUB, LANES), F32)
    return pl.pallas_call(
        body,
        in_specs=[smem] * 4 + [vmem] * len(arrays) + [hbm, vmem],
        out_specs=(vmem, vmem, vmem, hbm),
        out_shape=(
            half_shape, half_shape, pltpu.VMEM((NB * SUB, LANES), F32), jax.ShapeDtypeStruct(end.shape, F32),
        ),
        scratch_shapes=[
            pltpu.VMEM((sources, STEPS * ROWS, factors), BF16),
            pltpu.VMEM((factors * PITCH, LANES), F32),
            pltpu.VMEM((wide * PITCH, LANES), F32),
            pltpu.VMEM((wide * PITCH, LANES), F32),
            pltpu.VMEM((NB, SUB, LANES), F32),
            pltpu.VMEM(gd.shape, BF16),
            pltpu.VMEM((counterparties, SUB, LANES), F32),
            pltpu.SemaphoreType.DMA(()),
            pltpu.SemaphoreType.DMA(()),
        ],
        compiler_params=pltpu.CompilerParams(vmem_limit_bytes=40 * 1024 * 1024),
        name="revalue",
    )(
        slots, lists, currency, owner,
        *[on_chip(a) for a in arrays],
        pltpu.with_memory_space_constraint(gd, pltpu.HBM),
        on_chip(end),
    )


def basis_rows(base, s):
    row = lax.broadcasted_iota(jnp.int32, (NBP - NB, LANES), 0)
    one = jnp.where(row == 0, 1.0, 0.0).astype(F32)
    return jnp.concatenate([base[pl.ds(s, NB, stride=SUB), :], one], axis=0)


def moments_of(parts, base, paths):
    chunks = SUB // STEPS

    def body(p_ref, b_ref, net_ref, out_ref):
        net_ref[...] = jnp.sum(p_ref[...], axis=0)
        pad = jnp.zeros((LANES - NBP, chunks * LANES), F32)
        m = []
        for t in range(STEPS):
            right, mine = [], []
            for q in range(chunks):
                s = t * chunks + q
                right.append(basis_rows(b_ref, s))
                mine.append(net_ref[pl.ds(s, SUB, stride=SUB), :])
            right = jnp.concatenate(right, axis=1)
            left = jnp.concatenate([right, jnp.concatenate(mine, axis=1)], axis=0)
            m.append(lax.dot_general(
                left, jnp.concatenate([right, pad], axis=0), (((1,), (1,)), ((), ())),
                precision=HIGH, preferred_element_type=F32,
            ))
        low = jnp.concatenate([
            pltpu.roll(m[t][NBP:], 2 * NBP, 1) + pltpu.roll(m[t][NB:NBP], 3 * NBP, 1) for t in range(STEPS)
        ], axis=0)
        packed = m[0][:NB] + pltpu.roll(m[1][:NB], NBP, 1) + low
        for d in range(paths):
            out_ref[d] = packed

    return pl.pallas_call(
        body,
        in_specs=[VMEM_SPEC] * 2,
        out_specs=(VMEM_SPEC, VMEM_SPEC),
        out_shape=(
            pltpu.VMEM((SUB * SUB, LANES), F32),
            pltpu.VMEM((paths, NB, LANES), F32),
        ),
        name="moments",
    )(on_chip(parts), on_chip(base))


def expose(payload, net, base, total):
    chunks = SUB // STEPS

    def body(p_ref, n_ref, b_ref, o_hbm, o_ref, sem):
        acc = jnp.sum(p_ref[...], axis=0) * (1.0 / total)
        row = lax.broadcasted_iota(jnp.int32, (NBP + SUB, LANES), 0)
        lane = lax.broadcasted_iota(jnp.int32, (NBP + SUB, LANES), 1)
        diag = jnp.where((row == lane) & (row <= NB), 0.001, 0.0)
        sys = []
        for t in range(STEPS):
            rest = acc[t * SUB:(t + 1) * SUB]
            a = jnp.concatenate([
                acc if t == 0 else pltpu.roll(acc, LANES - NBP, 1),
                pltpu.roll(rest, LANES - 3 * NBP, 1),
                pltpu.roll(rest, LANES - 2 * NBP, 1),
            ], axis=0)
            sys.append(jnp.where(lane < NBP, a, 0.0) + diag)
        at = lax.broadcasted_iota(jnp.int32, (NBP, LANES), 0)
        col = lax.broadcasted_iota(jnp.int32, (NBP, LANES), 1)
        rows = []
        for t in range(STEPS):
            turned = jnp.transpose(sys[t][NBP:])[:NBP]
            rows.append(
                [jnp.broadcast_to(sys[t][:NBP, i:i + 1], (NBP, LANES)) for i in range(NB + 1)]
                + [jnp.broadcast_to(turned[:, c:c + 1], (NBP, LANES)) for c in range(SUB)]
            )
        for k in range(NB + 1):
            for t in range(STEPS):
                v = rows[t]
                inv = 1.0 / v[k][k:k + 1]
                w = v[k] * inv
                for i in range(k + 1, len(v)):
                    mine = v[i][k:k + 1]
                    v[i] = jnp.where(at == k, mine * inv, v[i] - mine * w)
        for t in range(STEPS):
            coef = jnp.zeros((NBP, LANES), F32)
            for c in range(SUB):
                coef = jnp.where(col == c, rows[t][NB + 1 + c], coef)
            steps = [t * chunks + q for q in range(chunks)]
            fitted = lax.dot_general(
                coef, jnp.concatenate([basis_rows(b_ref, s) for s in steps], axis=1), (((0,), (0,)), ((), ())),
                precision=HIGH, preferred_element_type=F32,
            )[:SUB]
            n = jnp.concatenate([n_ref[pl.ds(s, SUB, stride=SUB), :] for s in steps], axis=1)
            o_ref[t] = jnp.maximum(n - 0.9 * fitted, 0.0)
        cp = pltpu.make_async_copy(o_ref, o_hbm, sem)
        cp.start()
        cp.wait()

    return pl.pallas_call(
        body,
        in_specs=[VMEM_SPEC] * 3,
        out_specs=pl.BlockSpec(memory_space=pltpu.HBM),
        out_shape=jax.ShapeDtypeStruct((STEPS, SUB, chunks * LANES), F32),
        scratch_shapes=[pltpu.VMEM((STEPS, SUB, chunks * LANES), F32), pltpu.SemaphoreType.DMA(())],
        name="expose",
    )(on_chip(payload), on_chip(net), on_chip(base))


def evolve(start_state, shocks, loading, decay):
    rows, factors = start_state.shape
    parts = 8
    deep = factors // parts

    def body(z_hbm, l_hbm, s_hbm, d_hbm, slab_ref, end_ref, z, l, s, d, sem, lsem):
        small = [
            pltpu.make_async_copy(z_hbm, z, sem.at[0]),
            pltpu.make_async_copy(s_hbm, s, sem.at[1]),
            pltpu.make_async_copy(d_hbm, d, sem.at[2]),
        ]
        large = [
            pltpu.make_async_copy(l_hbm.at[pl.ds(i * deep, deep)], l.at[pl.ds(i * deep, deep)], lsem.at[i])
            for i in range(parts)
        ]
        for cp in small[:1] + large + small[1:]:
            cp.start()
        small[0].wait()
        moved = jnp.zeros((STEPS * rows, factors), F32)
        for i in range(parts):
            large[i].wait()
            moved = moved + jnp.dot(
                z[:, i * deep:(i + 1) * deep], l[pl.ds(i * deep, deep), :], preferred_element_type=F32
            )
        for cp in small[1:]:
            cp.wait()
        first = d[...] * s[...] + moved[:rows]
        end = d[...] * first + moved[rows:]
        end_ref[...] = end
        slab_ref[...] = jnp.concatenate([first, end], axis=0).astype(BF16)

    hbm = pl.BlockSpec(memory_space=pltpu.HBM)
    vmem = pl.BlockSpec(memory_space=pltpu.VMEM)
    args = (shocks.reshape(STEPS * rows, factors), loading, start_state, decay.reshape(1, factors))
    return pl.pallas_call(
        body,
        in_specs=[hbm] * 4,
        out_specs=(vmem, vmem),
        out_shape=(
            pltpu.VMEM((STEPS * rows, factors), BF16),
            pltpu.VMEM((rows, factors), F32),
        ),
        scratch_shapes=[
            pltpu.VMEM((STEPS * rows, factors), BF16),
            pltpu.VMEM((factors, factors), BF16),
            pltpu.VMEM((rows, factors), F32),
            pltpu.VMEM((1, factors), F32),
            pltpu.SemaphoreType.DMA((3,)),
            pltpu.SemaphoreType.DMA((parts,)),
        ],
        compiler_params=pltpu.CompilerParams(vmem_limit_bytes=24 * 1024 * 1024),
        name="evolve",
    )(*[pltpu.with_memory_space_constraint(a, pltpu.HBM) for a in args])


def per_device(start_state, shocks, loading, decay, factor_lists, delta, gamma, currency, owner):
    member = lax.axis_index("set")
    core, px, py = member % 2, (member // 2) % GRID, member // (2 * GRID)
    sets, depth = factor_lists.shape
    total = ROWS * lax.axis_size("set") * lax.axis_size("path")
    slab, state = evolve(start_state, shocks, loading, decay)

    line = [slab] + [lax.ppermute(slab, "set", hop_pairs(h, 0)) for h in HOPS[1:]]
    line = jnp.concatenate(line, axis=0)
    plane = [line] + [lax.ppermute(line, "set", hop_pairs(h, 1)) for h in HOPS[1:]]
    other = [lax.ppermute(a, "set", core_pairs()) for a in plane]

    hops = jnp.array(HOPS, jnp.int32)
    near, far = hops[None, :], hops[:, None]

    def slots_of(c):
        dx = jnp.where(c == 0, near, far)
        dy = jnp.where(c == 0, far, near)
        return (((py - dy) % GRID * GRID + (px - dx) % GRID) * 2 + c).reshape(-1)

    slots = jnp.concatenate([slots_of(core), slots_of(1 - core)]).astype(jnp.int32)
    lists = (factor_lists * PITCH).reshape(sets // NG, NG * depth).T.reshape(-1)
    place = jnp.where((owner // SUB) % 2 == core, 0, 128) + owner // (2 * SUB) * SUB + owner % SUB

    gd = prepare(gamma, delta)
    mine, theirs, base, state = revalue(
        slots, lists, currency, place, plane + other, gd, state, sets, depth
    )
    mine = mine + lax.ppermute(theirs, "set", core_pairs())
    chips = [[i * 2 + c for i in range(GRID * GRID)] for c in range(2)]
    parts = lax.all_to_all(
        mine.reshape(GRID * GRID, SUB * SUB, LANES), "set", 0, 0, axis_index_groups=chips
    )
    net, payload = moments_of(parts, base, lax.axis_size("path"))
    payload = lax.all_to_all(payload, "path", 0, 0)
    return expose(payload, net, base, total), state


def solution(mesh):
    return jax.shard_map(
        per_device,
        mesh=mesh,
        in_specs=(
            P(("path", "set"), None),
            P(None, ("path", "set"), None),
            P(),
            P(),
            P("set", None),
            P("set", None),
            P("set", None, None),
            P("set"),
            P("set"),
        ),
        out_specs=(P(None, "set", "path"), P(("path", "set"), None)),
        check_vma=False,
    )
```
